256 devices in a mesh: cand: 32 (over y, z), tp: 8 (over x, core).
Axes of the slice: x: 4, y: 4, z: 8, core: 2. Of those that a mesh axis runs over, the one named last changes fastest.
Arguments:
- reward_query: bfloat16 [256, 32, 8192], P('cand', None, 'tp'), may hold values from -170 to 170
- reward_new: bfloat16 [256, 2, 32, 1024], P('cand', None, None, 'tp'), may hold values from -7 to 7
- reward_key_value_cache: bfloat16 [256, 2, 768, 1024], P('cand', None, None, 'tp'), may hold values from -6 to 6
- reward_length: int32 [256], P('cand'), may hold values from 1 to 768
- out_weight: bfloat16 [8192, 4096], P('tp'), may hold values from -0.09375 to 0.09375
- policy_cache: bfloat16 [256, 2, 768, 1024], P('cand', None, None, 'tp'), may hold values from -6 to 6
- policy_length: int32 [256], replicated, may hold values from 1 to 767
- source: int32 [128], replicated, may hold values from 0 to 255, as said below
- policy_query: bfloat16 [128, 8192], P('cand', 'tp'), may hold values from -170 to 170
- policy_new: bfloat16 [128, 2, 1024], P('cand', None, 'tp'), may hold values from -7 to 7
Outputs:
- reward_out: bfloat16 [8192, 4096], P('cand', 'tp')
- compacted: bfloat16 [128, 2, 768, 1024], P('cand', None, None, 'tp')
- policy_attn: bfloat16 [128, 8192], P('cand', 'tp')
The draws below stay inside these ranges and needn't reach their ends.
Inputs may be any that keep to these rules, and one draw needn't show every extreme that they name: `source`: distinct candidate indices; the 8 candidates of each index of cand are named exactly 4 times.
All inputs are finite; a program needn't handle non-finite values.
Results may differ from the reference program's by a relative error of at most 0.0057.
Values may be sent and summed in bfloat16 or wider, within the bound.
A program may use at most 128 MiB of HBM per device.

```python
import jax
import jax.numpy as jnp
from jax import lax

ASKING_UNITS = 64
SHARED_KV_UNITS = 8
ATTN_DIM = 128
DOUT = 4096
NEW_TOKEN_COUNT = 32
CACHE_LENGTH = 768
CPG = 8
SLOT_DEV = 4
CANDIDATE_COUNT = 256
RETAINED_TOTAL = 128


def truncated_gaussian(key, tag, shape):
    return jnp.clip(jax.random.normal(jax.random.fold_in(key, tag), shape, jnp.float32), -6.0, 6.0)


def prefix_entries(key):
    return truncated_gaussian(key, 42, (CANDIDATE_COUNT, SHARED_KV_UNITS * ATTN_DIM))


def chosen_parents(key):
    group_count = CANDIDATE_COUNT // CPG
    group_keys = jax.random.split(jax.random.fold_in(key, 51), group_count)
    orders = jax.vmap(lambda one_key: jax.random.permutation(one_key, CPG))(group_keys)
    retained_entries = orders[:, :SLOT_DEV] + (jnp.arange(group_count, dtype=jnp.int32) * CPG)[:, None]
    retained_entries = retained_entries.reshape(RETAINED_TOTAL).astype(jnp.int32)
    return jax.random.permutation(jax.random.fold_in(key, 52), retained_entries).astype(jnp.int32)


def draw_reward_new(key, part):
    appended_symbols = truncated_gaussian(key, 31, (CANDIDATE_COUNT, 2, NEW_TOKEN_COUNT, SHARED_KV_UNITS * ATTN_DIM))
    return appended_symbols.astype(jnp.bfloat16)


def draw_reward_query(key, part):
    probe_entries = truncated_gaussian(key, 32, (CANDIDATE_COUNT, NEW_TOKEN_COUNT, ASKING_UNITS * ATTN_DIM))
    return probe_entries.astype(jnp.bfloat16)


def draw_reward_length(key, part):
    drawn = jax.random.randint(jax.random.fold_in(key, 61), (CANDIDATE_COUNT,), 1, CACHE_LENGTH + 1)
    marked = jax.random.randint(jax.random.fold_in(key, 62), (), 0, CANDIDATE_COUNT)
    return jnp.where(jnp.arange(CANDIDATE_COUNT) == marked, CACHE_LENGTH, drawn).astype(jnp.int32)


def draw_policy_length(key, part):
    drawn = jax.random.randint(jax.random.fold_in(key, 63), (CANDIDATE_COUNT,), 1, CACHE_LENGTH)
    marked = jax.random.randint(jax.random.fold_in(key, 64), (), 0, CANDIDATE_COUNT)
    return jnp.where(jnp.arange(CANDIDATE_COUNT) == marked, CACHE_LENGTH - 1, drawn).astype(jnp.int32)


def draw_source(key, part):
    return chosen_parents(key)


def draw_policy_cache(key, part):
    layer_cache = truncated_gaussian(key, 41, (CANDIDATE_COUNT, 2, CACHE_LENGTH, SHARED_KV_UNITS * ATTN_DIM))
    layer_cache = layer_cache.at[:, 0, 0, :].set(prefix_entries(key))
    return layer_cache.astype(jnp.bfloat16)


def draw_policy_query(key, part):
    probe_entries = truncated_gaussian(key, 43, (RETAINED_TOTAL, ASKING_UNITS * ATTN_DIM))
    return probe_entries.astype(jnp.bfloat16)


def draw_policy_new(key, part):
    appended_symbols = truncated_gaussian(key, 44, (RETAINED_TOTAL, 2, SHARED_KV_UNITS * ATTN_DIM))
    return appended_symbols.astype(jnp.bfloat16)


def with_spikes(entries, rng, source, target, parts, factor):
    def block_of(axis_at):
        return (jnp.arange(entries.shape[axis_at]) // (entries.shape[axis_at] // parts)).reshape((-1,) + (1,) * (entries.ndim - 1 - axis_at))

    one_side = jax.random.permutation(rng, parts)[block_of(target)]
    far = (block_of(target) + parts // 2) % parts
    return jnp.where((block_of(source) == one_side) | (block_of(source) == far), factor * entries, entries)


def steps_of(stream_key, dims, pieces, low, largest):
    factor_of, own = 1.0, jax.random.fold_in(stream_key, 6)
    for axis_at, parts in pieces:
        heights = jnp.exp(jax.random.uniform(jax.random.fold_in(own, axis_at), (parts,), jnp.float32, low / len(pieces), largest / len(pieces)))
        factor_of = factor_of * jnp.repeat(heights, dims[axis_at] // parts).reshape([-1 if axis == axis_at else 1 for axis in range(len(dims))])
    return factor_of


def gaussian(key, extent, width, bound, cuts=(), kind=jnp.bfloat16):
    values = width * jax.random.normal(key, extent, jnp.float32)
    if cuts:
        values = values * steps_of(key, extent, cuts, -0.22, 0.18)
    return jnp.clip(values, -bound, bound).astype(kind)


def heavy_noise(stream_key, dims, deviation, limit, cuts, heavy, held_as=jnp.bfloat16):
    entries = deviation * jax.random.normal(stream_key, dims, jnp.float32)
    if cuts:
        entries = entries * steps_of(stream_key, dims, cuts, -0.22, 0.18)
    return jnp.clip(with_spikes(entries, jax.random.fold_in(stream_key, 3), *heavy), -limit, limit).astype(held_as)


def setup_inputs(seed: int = 0) -> dict:
    key_of = jax.random.split(jax.random.key(seed), 11)
    return {
        "reward_query": draw_reward_query(jax.random.fold_in(key_of[10], 71), 0),
        "reward_new": draw_reward_new(jax.random.fold_in(key_of[10], 71), 0),
        "reward_key_value_cache": gaussian(key_of[2], (CANDIDATE_COUNT, 2, CACHE_LENGTH, SHARED_KV_UNITS * ATTN_DIM), 1.0, 6.0, ((0, 32), (3, 8))),
        "reward_length": draw_reward_length(jax.random.fold_in(key_of[10], 71), 0),
        "out_weight": heavy_noise(key_of[4], (ASKING_UNITS * ATTN_DIM, DOUT), (ASKING_UNITS * ATTN_DIM) ** -0.5, 0.09375, ((0, 8),), (0, 1, 8, 2.0)),
        "policy_cache": draw_policy_cache(jax.random.fold_in(key_of[10], 71), 0),
        "policy_length": draw_policy_length(jax.random.fold_in(key_of[10], 71), 0),
        "source": draw_source(jax.random.fold_in(key_of[10], 71), 0),
        "policy_query": draw_policy_query(jax.random.fold_in(key_of[10], 71), 0),
        "policy_new": draw_policy_new(jax.random.fold_in(key_of[10], 71), 0),
    }


def reward_one(inputs):
    probe_entries, new_key_value, layer_cache, length = inputs
    attention_clusters = ASKING_UNITS // SHARED_KV_UNITS
    key_rows = jnp.concatenate([layer_cache[0], new_key_value[0]], axis=0).astype(jnp.float32).reshape(CACHE_LENGTH + NEW_TOKEN_COUNT, SHARED_KV_UNITS, ATTN_DIM)
    value_rows = jnp.concatenate([layer_cache[1], new_key_value[1]], axis=0).astype(jnp.float32).reshape(CACHE_LENGTH + NEW_TOKEN_COUNT, SHARED_KV_UNITS, ATTN_DIM)
    head_list = probe_entries.astype(jnp.float32).reshape(NEW_TOKEN_COUNT, SHARED_KV_UNITS, attention_clusters, ATTN_DIM)
    scores = jnp.einsum("tkgd,pkd->kgtp", head_list, key_rows) * (ATTN_DIM ** -0.5)
    position = jnp.arange(CACHE_LENGTH + NEW_TOKEN_COUNT, dtype=jnp.int32)
    token = jnp.arange(NEW_TOKEN_COUNT, dtype=jnp.int32)
    visible = (position[None, :] < length) | ((position[None, :] >= CACHE_LENGTH) & (position[None, :] - CACHE_LENGTH <= token[:, None]))
    scores = jnp.where(visible, scores, -1e30)
    weights = jax.nn.softmax(scores, axis=-1).astype(jnp.bfloat16)
    mixed = jnp.einsum("kgtp,pkd->tkgd", weights.astype(jnp.float32), value_rows)
    return mixed.reshape(NEW_TOKEN_COUNT, ASKING_UNITS * ATTN_DIM).astype(jnp.bfloat16)


def policy_one(inputs):
    probe_entries, layer_cache, length = inputs
    attention_clusters = ASKING_UNITS // SHARED_KV_UNITS
    key_rows = layer_cache[0].astype(jnp.float32).reshape(CACHE_LENGTH, SHARED_KV_UNITS, ATTN_DIM)
    value_rows = layer_cache[1].astype(jnp.float32).reshape(CACHE_LENGTH, SHARED_KV_UNITS, ATTN_DIM)
    head_list = probe_entries.astype(jnp.float32).reshape(SHARED_KV_UNITS, attention_clusters, ATTN_DIM)
    scores = jnp.einsum("kgd,pkd->kgp", head_list, key_rows) * (ATTN_DIM ** -0.5)
    position = jnp.arange(CACHE_LENGTH, dtype=jnp.int32)
    scores = jnp.where(position <= length, scores, -1e30)
    weights = jax.nn.softmax(scores, axis=-1).astype(jnp.bfloat16)
    mixed = jnp.einsum("kgp,pkd->kgd", weights.astype(jnp.float32), value_rows)
    return mixed.reshape(ASKING_UNITS * ATTN_DIM).astype(jnp.bfloat16)


def reference(reward_query, reward_new, reward_key_value_cache, reward_length, out_weight, policy_cache, policy_length, source, policy_query, policy_new):
    attn_rows = lax.map(reward_one, (reward_query, reward_new, reward_key_value_cache, reward_length))
    attn_rows = attn_rows.reshape(CANDIDATE_COUNT * NEW_TOKEN_COUNT, ASKING_UNITS * ATTN_DIM)
    reward_out = jnp.dot(attn_rows, out_weight, preferred_element_type=jnp.float32).astype(jnp.bfloat16)
    moved = policy_cache[source]
    slot_lengths = policy_length[source].astype(jnp.int32)
    position = jnp.arange(CACHE_LENGTH, dtype=jnp.int32)
    compacted = jnp.where(position[None, None, :, None] == slot_lengths[:, None, None, None], policy_new[:, :, None, :], moved)
    policy_attn = lax.map(policy_one, (policy_query, compacted, slot_lengths))
    return reward_out, compacted, policy_attn
```

```python
import jax
import jax.numpy as jnp
from jax import lax
from jax.sharding import PartitionSpec as P

ASKING_UNITS = 64
SHARED_KV_UNITS = 8
ATTN_DIM = 128
NEW_TOKEN_COUNT = 32
CACHE_LENGTH = 768


def body(
    reward_query,
    reward_new,
    reward_key_value_cache,
    reward_length,
    out_weight,
    policy_cache,
    policy_length,
    source,
    policy_query,
    policy_new,
):
    attention_clusters = ASKING_UNITS // SHARED_KV_UNITS
    score_scale = ATTN_DIM ** (-0.5)
    count = reward_query.shape[0]
    kv_heads = reward_key_value_cache.shape[-1] // ATTN_DIM
    head_list = reward_query.reshape(count, NEW_TOKEN_COUNT, kv_heads, attention_clusters, ATTN_DIM)
    cache_keys = reward_key_value_cache[:, 0].reshape(count, CACHE_LENGTH, kv_heads, ATTN_DIM)
    cache_values = reward_key_value_cache[:, 1].reshape(count, CACHE_LENGTH, kv_heads, ATTN_DIM)
    fresh_keys = reward_new[:, 0].reshape(count, NEW_TOKEN_COUNT, kv_heads, ATTN_DIM)
    fresh_values = reward_new[:, 1].reshape(count, NEW_TOKEN_COUNT, kv_heads, ATTN_DIM)
    old_scores = (
        jnp.einsum("ctkgd,cpkd->ckgtp", head_list, cache_keys, preferred_element_type=jnp.float32)
        * score_scale
    )
    new_scores = (
        jnp.einsum("ctkgd,cukd->ckgtu", head_list, fresh_keys, preferred_element_type=jnp.float32)
        * score_scale
    )
    cache_rows = lax.iota(jnp.int32, CACHE_LENGTH)
    old_visible = cache_rows[None, :] < reward_length[:, None]
    old_scores = jnp.where(old_visible[:, None, None, None, :], old_scores, -1e30)
    token_rows = lax.iota(jnp.int32, NEW_TOKEN_COUNT)
    new_visible = token_rows[None, :] <= token_rows[:, None]
    new_scores = jnp.where(new_visible, new_scores, -1e30)
    peak = jnp.maximum(old_scores.max(-1), new_scores.max(-1))[..., None]
    old_exp = jnp.exp(old_scores - peak)
    new_exp = jnp.exp(new_scores - peak)
    denominator = old_exp.sum(-1, keepdims=True) + new_exp.sum(-1, keepdims=True)
    old_weights = (old_exp / denominator).astype(jnp.bfloat16)
    new_weights = (new_exp / denominator).astype(jnp.bfloat16)
    mixed = jnp.einsum(
        "ckgtp,cpkd->ctkgd", old_weights, cache_values, preferred_element_type=jnp.float32
    )
    mixed = mixed + jnp.einsum(
        "ckgtu,cukd->ctkgd", new_weights, fresh_values, preferred_element_type=jnp.float32
    )
    attn_rows = mixed.reshape(
        count * NEW_TOKEN_COUNT, kv_heads * attention_clusters * ATTN_DIM
    ).astype(jnp.bfloat16)
    partial_value = jnp.dot(attn_rows, out_weight, preferred_element_type=jnp.float32)
    pieces = partial_value.astype(jnp.bfloat16).reshape(count * NEW_TOKEN_COUNT, 8, -1)
    pieces = lax.all_to_all(
        pieces.transpose(1, 0, 2), "tp", split_axis=0, concat_axis=0, tiled=True
    )
    reward_out = pieces.astype(jnp.float32).sum(0).astype(jnp.bfloat16)
    slot_count = policy_query.shape[0]
    groups = source.shape[0] // slot_count
    me = lax.axis_index("cand")
    owner = source // count
    same = owner[:, None] == owner[None, :]
    slots = lax.iota(jnp.int32, source.shape[0])
    rank = jnp.sum(same & (slots[None, :] < slots[:, None]), axis=1)
    mine = (owner == me)[None, :] & (rank[None, :] == lax.iota(jnp.int32, slot_count)[:, None])
    picked = jnp.sum(jnp.where(mine, (source % count)[None, :], 0), axis=1)
    total_rows = 2 * CACHE_LENGTH
    chunk = total_rows // groups
    leaving = jnp.take(policy_cache.reshape(count, groups, chunk, ATTN_DIM), picked, axis=0)
    leaving = leaving.transpose(1, 0, 2, 3)
    spread = lax.all_to_all(leaving, "cand", split_axis=0, concat_axis=0, tiled=True)
    spread = spread.reshape(groups * slot_count, chunk, ATTN_DIM)
    selected = jnp.take(spread, owner * slot_count + rank, axis=0)
    selected = selected.reshape(groups, slot_count, chunk, ATTN_DIM)
    moved = lax.all_to_all(selected, "cand", split_axis=0, concat_axis=0, tiled=True)
    moved = moved.transpose(1, 0, 2, 3).reshape(slot_count, 2, CACHE_LENGTH, ATTN_DIM)
    local_source = lax.dynamic_slice_in_dim(source, me * slot_count, slot_count)
    slot_lengths = jnp.take(policy_length, local_source)
    compacted = jnp.where(
        cache_rows[None, None, :, None] == slot_lengths[:, None, None, None],
        policy_new[:, :, None, :],
        moved,
    )
    slot_heads = policy_query.reshape(slot_count, kv_heads, attention_clusters, ATTN_DIM)
    slot_keys = compacted[:, 0].reshape(slot_count, CACHE_LENGTH, kv_heads, ATTN_DIM)
    slot_values = compacted[:, 1].reshape(slot_count, CACHE_LENGTH, kv_heads, ATTN_DIM)
    slot_scores = (
        jnp.einsum("skgd,spkd->skgp", slot_heads, slot_keys, preferred_element_type=jnp.float32)
        * score_scale
    )
    slot_visible = cache_rows[None, :] <= slot_lengths[:, None]
    slot_scores = jnp.where(slot_visible[:, None, None, :], slot_scores, -1e30)
    slot_weights = jax.nn.softmax(slot_scores, axis=-1).astype(jnp.bfloat16)
    policy_attn = jnp.einsum(
        "skgp,spkd->skgd", slot_weights, slot_values, preferred_element_type=jnp.float32
    )
    policy_attn = policy_attn.reshape(slot_count, kv_heads * attention_clusters * ATTN_DIM).astype(
        jnp.bfloat16
    )
    return (reward_out, compacted, policy_attn)


def solution(mesh):
    in_specs = (
        P("cand", None, "tp"),
        P("cand", None, None, "tp"),
        P("cand", None, None, "tp"),
        P("cand"),
        P("tp", None),
        P("cand", None, None, "tp"),
        P(),
        P(),
        P("cand", "tp"),
        P("cand", None, "tp"),
    )
    out_specs = (P("cand", "tp"), P("cand", None, None, "tp"), P("cand", "tp"))
    return jax.shard_map(body, mesh=mesh, in_specs=in_specs, out_specs=out_specs, check_vma=False)
```

```python
import functools

import jax
import jax.numpy as jnp
from jax import lax
from jax.experimental import pallas as pl
from jax.experimental.pallas import tpu as pltpu
from jax.sharding import PartitionSpec as P

ASKING_UNITS = 64
SHARED_KV_UNITS = 8
ATTN_DIM = 128
NEW_TOKEN_COUNT = 32
CACHE_LENGTH = 768
PER_KV = ASKING_UNITS // SHARED_KV_UNITS
ROWS = 2 * CACHE_LENGTH
SCALE = ATTN_DIM ** (-0.5)
PARTS = 3


def score(rows, keys):
    return lax.dot_general(
        rows, keys, (((1,), (1,)), ((), ())), preferred_element_type=jnp.float32
    )


def exchange_kernel(
    groups,
    shares,
    slots,
    picked,
    chosen,
    lengths,
    query_hbm,
    new_hbm,
    kv_hbm,
    weight_hbm,
    cache_hbm,
    out_ref,
    moved_ref,
    cache,
    leaving,
    arrived0,
    arrived1,
    arrived2,
    sorted_rows,
    query,
    new,
    kv,
    weight,
    attn,
    pieces,
    others,
    load_sem,
    send1,
    recv1,
    send2,
    recv2,
    send3,
    recv3,
    own_sem,
):
    arrived = (arrived0, arrived1, arrived2)
    me = lax.axis_index("cand")
    share = lax.axis_index("tp")
    chunk = ROWS // groups
    part = chunk // PARTS
    count = query.shape[0]
    width = pieces.shape[2]

    loads = [
        pltpu.make_async_copy(cache_hbm, cache, load_sem.at[0]),
        pltpu.make_async_copy(query_hbm, query, load_sem.at[1]),
        pltpu.make_async_copy(new_hbm, new, load_sem.at[2]),
        pltpu.make_async_copy(kv_hbm, kv, load_sem.at[3]),
        pltpu.make_async_copy(weight_hbm, weight, load_sem.at[4]),
    ]
    for load in loads:
        load.start()

    barrier = pltpu.get_barrier_semaphore()

    @pl.loop(1, groups)
    def _(i):
        pl.semaphore_signal(barrier, inc=1, device_id={"cand": lax.rem(me + i, groups)})

    @pl.loop(1, shares)
    def _(i):
        pl.semaphore_signal(barrier, inc=1, device_id={"tp": lax.rem(share + i, shares)})

    loads[0].wait()
    step = 128

    @pl.loop(0, ROWS // step)
    def _(i):
        rows = pl.ds(pl.multiple_of(i * step, step), step)
        for k in range(slots):
            leaving[k, rows, :] = cache[picked[k], rows, :]

    pl.semaphore_wait(barrier, groups + shares - 2)

    def first(h, i):
        peer = lax.rem(me + i, groups)
        rows = pl.ds(pl.multiple_of(peer * chunk + h * part, part), part)
        return pltpu.make_async_remote_copy(
            src_ref=leaving.at[:, rows, :],
            dst_ref=arrived[h].at[pl.ds(i * slots, slots)],
            send_sem=send1.at[h],
            recv_sem=recv1.at[h],
            device_id={"cand": peer},
        )

    for h in range(PARTS):

        @pl.loop(1, groups)
        def _(t):
            first(h, lax.rem(t * 5, groups)).start()

        rows = pl.ds(pl.multiple_of(me * chunk + h * part, part), part)
        for k in range(slots):
            arrived[h][k] = leaving[k, rows, :]

    for load in loads[1:4]:
        load.wait()
    lead = PER_KV * NEW_TOKEN_COUNT
    tokens = lax.broadcasted_iota(jnp.int32, (lead, NEW_TOKEN_COUNT), 0) % NEW_TOKEN_COUNT
    fresh = lax.broadcasted_iota(jnp.int32, (lead, NEW_TOKEN_COUNT), 1) <= tokens
    place = lax.broadcasted_iota(jnp.int32, (lead, CACHE_LENGTH), 1)

    @pl.loop(0, count)
    def _(c):
        heads = jnp.concatenate(
            [query[c, :, g * ATTN_DIM : (g + 1) * ATTN_DIM] for g in range(PER_KV)], axis=0
        )
        old = jnp.where(place < lengths[c], score(heads, kv[c, 0]) * SCALE, -1e30)
        now = jnp.where(fresh, score(heads, new[c, 0]) * SCALE, -1e30)
        peak = jnp.maximum(old.max(-1, keepdims=True), now.max(-1, keepdims=True))
        old = jnp.exp(old - peak)
        now = jnp.exp(now - peak)
        inverse = 1.0 / (old.sum(-1, keepdims=True) + now.sum(-1, keepdims=True))
        mixed = jnp.dot(
            (old * inverse).astype(jnp.bfloat16), kv[c, 1], preferred_element_type=jnp.float32
        ) + jnp.dot(
            (now * inverse).astype(jnp.bfloat16), new[c, 1], preferred_element_type=jnp.float32
        )
        mixed = mixed.astype(jnp.bfloat16)
        rows = pl.ds(pl.multiple_of(c * NEW_TOKEN_COUNT, NEW_TOKEN_COUNT), NEW_TOKEN_COUNT)
        for g in range(PER_KV):
            attn[rows, g * ATTN_DIM : (g + 1) * ATTN_DIM] = mixed[
                g * NEW_TOKEN_COUNT : (g + 1) * NEW_TOKEN_COUNT
            ]

    loads[4].wait()

    @pl.loop(0, shares)
    def _(p):
        columns = pl.ds(pl.multiple_of(p * width, width), width)
        pieces[p] = jnp.dot(
            attn[...], weight[:, columns], preferred_element_type=jnp.float32
        ).astype(jnp.bfloat16)

    def across(i):
        peer = lax.rem(share + i, shares)
        return pltpu.make_async_remote_copy(
            src_ref=pieces.at[peer],
            dst_ref=others.at[i - 1],
            send_sem=send3,
            recv_sem=recv3,
            device_id={"tp": peer},
        )

    @pl.loop(1, shares)
    def _(i):
        across(i).start()

    def second(h, i):
        peer = lax.rem(me + i, groups)
        rows = pl.ds(pl.multiple_of(me * chunk + h * part, part), part)
        return pltpu.make_async_remote_copy(
            src_ref=sorted_rows.at[pl.ds((h * groups + peer) * slots, slots)],
            dst_ref=moved_ref.at[:, rows, :],
            send_sem=send2,
            recv_sem=recv2,
            device_id={"cand": peer},
        )

    def keep(h):
        rows = pl.ds(pl.multiple_of(me * chunk + h * part, part), part)
        return pltpu.make_async_copy(
            sorted_rows.at[pl.ds((h * groups + me) * slots, slots)],
            moved_ref.at[:, rows, :],
            own_sem.at[h],
        )

    incoming = (groups - 1) * slots
    for h in range(PARTS):
        pltpu.make_async_copy(
            arrived[h].at[pl.ds(0, incoming)], arrived[h].at[pl.ds(slots, incoming)], recv1.at[h]
        ).wait()

        @pl.loop(0, groups)
        def _(g):
            for k in range(slots):
                s = g * slots + k
                sorted_rows[h * groups * slots + s] = arrived[h][chosen[s]]

        @pl.loop(1, groups)
        def _(t):
            second(h, lax.rem(t * 5, groups)).start()

        keep(h).start()

    pltpu.make_async_copy(others, others, recv3).wait()
    block = 32

    @pl.loop(0, out_ref.shape[0] // block)
    def _(r):
        rows = pl.ds(pl.multiple_of(r * block, block), block)
        total = pieces[share, rows, :].astype(jnp.float32)
        for i in range(shares - 1):
            total = total + others[i, rows, :].astype(jnp.float32)
        out_ref[rows, :] = total.astype(jnp.bfloat16)

    pltpu.make_async_copy(others, others, send3).wait()
    for h in range(PARTS):
        pltpu.make_async_copy(
            arrived[h].at[pl.ds(0, incoming)], arrived[h].at[pl.ds(slots, incoming)], send1.at[h]
        ).wait()
        keep(h).wait()
    everything = PARTS * incoming
    for sem in (send2, recv2):
        pltpu.make_async_copy(
            sorted_rows.at[pl.ds(0, everything)], sorted_rows.at[pl.ds(0, everything)], sem
        ).wait()


def exchange(groups, shares, slots, picked, chosen, lengths, query, new, kv, weight, cache):
    count = query.shape[0]
    chunk = ROWS // groups
    part = chunk // PARTS
    bf16 = jnp.bfloat16
    width = weight.shape[1] // shares
    lead = count * NEW_TOKEN_COUNT
    smem = pl.BlockSpec(memory_space=pltpu.SMEM)
    anywhere = pl.BlockSpec(memory_space=pl.ANY)
    dma = pltpu.SemaphoreType.DMA
    return pl.pallas_call(
        functools.partial(exchange_kernel, groups, shares, slots),
        out_shape=(
            jax.ShapeDtypeStruct((lead, width), bf16),
            jax.ShapeDtypeStruct((slots, ROWS, ATTN_DIM), bf16),
        ),
        in_specs=[smem] * 3 + [anywhere] * 5,
        out_specs=(pl.BlockSpec(memory_space=pltpu.VMEM), anywhere),
        scratch_shapes=[
            pltpu.VMEM((count, ROWS, ATTN_DIM), bf16),
            pltpu.VMEM((slots, ROWS, ATTN_DIM), bf16),
            pltpu.VMEM((groups * slots, part, ATTN_DIM), bf16),
            pltpu.VMEM((groups * slots, part, ATTN_DIM), bf16),
            pltpu.VMEM((groups * slots, part, ATTN_DIM), bf16),
            pltpu.VMEM((PARTS * groups * slots, part, ATTN_DIM), bf16),
            pltpu.VMEM(query.shape, bf16),
            pltpu.VMEM(new.shape, bf16),
            pltpu.VMEM(kv.shape, bf16),
            pltpu.VMEM(weight.shape, bf16),
            pltpu.VMEM((lead, weight.shape[0]), bf16),
            pltpu.VMEM((shares, lead, width), bf16),
            pltpu.VMEM((shares - 1, lead, width), bf16),
            dma((5,)),
            dma((PARTS,)),
            dma((PARTS,)),
            dma,
            dma,
            dma,
            dma,
            dma((PARTS,)),
        ],
        compiler_params=pltpu.CompilerParams(
            collective_id=0, has_side_effects=True, vmem_limit_bytes=60 * 1024 * 1024
        ),
        name="exchange",
    )(picked, chosen, lengths, query, new, kv, weight, cache)


def policy_kernel(lengths, moved, new, query, kept, out, rows_out):
    s = pl.program_id(0)
    slots = query.shape[0]
    length = lengths[s]
    row = lax.broadcasted_iota(jnp.int32, (CACHE_LENGTH, ATTN_DIM), 0)
    keys = jnp.where(row == length, new[0, 0:1, :], moved[0, 0:CACHE_LENGTH, :])
    values = jnp.where(row == length, new[0, 1:2, :], moved[0, CACHE_LENGTH:ROWS, :])
    kept[0, 0] = keys
    kept[0, 1] = values
    which = lax.broadcasted_iota(jnp.int32, query.shape, 0)
    line = jnp.where(which == s, query[...].astype(jnp.float32), 0.0).sum(0, keepdims=True)
    heads = jnp.concatenate(
        [line[:, g * ATTN_DIM : (g + 1) * ATTN_DIM] for g in range(PER_KV)], axis=0
    ).astype(jnp.bfloat16)
    place = lax.broadcasted_iota(jnp.int32, (PER_KV, CACHE_LENGTH), 1)
    found = jnp.where(place <= length, score(heads, keys) * SCALE, -1e30)
    found = jnp.exp(found - found.max(-1, keepdims=True))
    found = found * (1.0 / found.sum(-1, keepdims=True))
    mixed = jnp.dot(found.astype(jnp.bfloat16), values, preferred_element_type=jnp.float32)
    line = jnp.concatenate([mixed[g : g + 1] for g in range(PER_KV)], axis=1)

    @pl.when(s == 0)
    def _():
        rows_out[...] = jnp.zeros_like(rows_out)

    rows_out[...] = jnp.where(which == s, line, rows_out[...])

    @pl.when(s == slots - 1)
    def _():
        out[...] = rows_out[...].astype(jnp.bfloat16)


def policy(lengths, moved, new, query):
    slots = query.shape[0]
    bf16 = jnp.bfloat16
    whole = pl.BlockSpec(query.shape, lambda s, lens: (0, 0))
    return pl.pallas_call(
        policy_kernel,
        out_shape=(
            jax.ShapeDtypeStruct((slots, 2, CACHE_LENGTH, ATTN_DIM), bf16),
            jax.ShapeDtypeStruct(query.shape, bf16),
        ),
        grid_spec=pltpu.PrefetchScalarGridSpec(
            num_scalar_prefetch=1,
            grid=(slots,),
            in_specs=[
                pl.BlockSpec((1, ROWS, ATTN_DIM), lambda s, lens: (s, 0, 0)),
                pl.BlockSpec((1, 2, ATTN_DIM), lambda s, lens: (s, 0, 0)),
                whole,
            ],
            out_specs=(
                pl.BlockSpec((1, 2, CACHE_LENGTH, ATTN_DIM), lambda s, lens: (s, 0, 0, 0)),
                whole,
            ),
            scratch_shapes=[pltpu.VMEM(query.shape, jnp.float32)],
        ),
        name="policy",
    )(lengths, moved, new, query)


def body(
    groups,
    shares,
    reward_query,
    reward_new,
    reward_key_value_cache,
    reward_length,
    out_weight,
    policy_cache,
    policy_length,
    source,
    policy_query,
    policy_new,
):
    count = reward_query.shape[0]
    slots = policy_query.shape[0]
    me = lax.axis_index("cand")
    owner = source // count
    same = owner[:, None] == owner[None, :]
    order = lax.iota(jnp.int32, source.shape[0])
    rank = jnp.sum(same & (order[None, :] < order[:, None]), axis=1)
    mine = (owner == me)[None, :] & (rank[None, :] == lax.iota(jnp.int32, slots)[:, None])
    picked = jnp.sum(jnp.where(mine, (source % count)[None, :], 0), axis=1)
    chosen = ((me - owner + groups) % groups) * slots + rank
    reward_out, moved = exchange(
        groups,
        shares,
        slots,
        picked,
        chosen,
        reward_length,
        reward_query,
        reward_new,
        reward_key_value_cache,
        out_weight,
        policy_cache.reshape(count, ROWS, ATTN_DIM),
    )
    local_source = lax.dynamic_slice_in_dim(source, me * slots, slots)
    slot_lengths = jnp.take(policy_length, local_source)
    compacted, policy_attn = policy(slot_lengths, moved, policy_new, policy_query)
    return (reward_out, compacted, policy_attn)


def solution(mesh):
    in_specs = (
        P("cand", None, "tp"),
        P("cand", None, None, "tp"),
        P("cand", None, None, "tp"),
        P("cand"),
        P("tp", None),
        P("cand", None, None, "tp"),
        P(),
        P(),
        P("cand", "tp"),
        P("cand", None, "tp"),
    )
    out_specs = (P("cand", "tp"), P("cand", None, None, "tp"), P("cand", "tp"))
    return jax.shard_map(
        functools.partial(body, mesh.shape["cand"], mesh.shape["tp"]),
        mesh=mesh,
        in_specs=in_specs,
        out_specs=out_specs,
        check_vma=False,
    )
```

```python
import functools

import jax
import jax.numpy as jnp
from jax import lax
from jax.experimental import pallas as pl
from jax.experimental.pallas import tpu as pltpu
from jax.sharding import PartitionSpec as P

ASKING_UNITS = 64
SHARED_KV_UNITS = 8
ATTN_DIM = 128
NEW_TOKEN_COUNT = 32
CACHE_LENGTH = 768
PER_KV = ASKING_UNITS // SHARED_KV_UNITS
ROWS = 2 * CACHE_LENGTH
SCALE = ATTN_DIM ** (-0.5)
PARTS = 3


def score(rows, keys):
    return lax.dot_general(
        rows, keys, (((1,), (1,)), ((), ())), preferred_element_type=jnp.float32
    )


def exchange_kernel(
    groups,
    shares,
    slots,
    chosen,
    lengths,
    query_hbm,
    new_hbm,
    kv_hbm,
    weight_hbm,
    cache_hbm,
    out_ref,
    moved_ref,
    cache0,
    cache1,
    cache2,
    leaving0,
    leaving1,
    leaving2,
    arrived0,
    arrived1,
    arrived2,
    sorted_rows,
    query,
    new,
    kv,
    weight,
    attn,
    pieces,
    others,
    span_sem,
    load_sem,
    send1,
    recv1,
    send2,
    recv2,
    send3,
    recv3,
    own_sem,
):
    cache = (cache0, cache1, cache2)
    leaving = (leaving0, leaving1, leaving2)
    arrived = (arrived0, arrived1, arrived2)
    me = lax.axis_index("cand")
    share = lax.axis_index("tp")
    span = ROWS // PARTS
    part = span // groups
    count = query.shape[0]
    width = pieces.shape[2]

    spans = [
        pltpu.make_async_copy(
            cache_hbm.at[:, pl.ds(h * span, span), :], cache[h], span_sem.at[h]
        )
        for h in range(PARTS)
    ]
    loads = [
        pltpu.make_async_copy(query_hbm, query, load_sem.at[0]),
        pltpu.make_async_copy(new_hbm, new, load_sem.at[1]),
        pltpu.make_async_copy(kv_hbm, kv, load_sem.at[2]),
        pltpu.make_async_copy(weight_hbm, weight, load_sem.at[3]),
    ]
    for load in spans:
        load.start()

    barrier = pltpu.get_barrier_semaphore()

    @pl.loop(1, groups)
    def _(i):
        pl.semaphore_signal(barrier, inc=1, device_id={"cand": lax.rem(me + i, groups)})

    @pl.loop(1, shares)
    def _(i):
        pl.semaphore_signal(barrier, inc=1, device_id={"tp": lax.rem(share + i, shares)})

    step = 128

    def pick(h):
        @pl.loop(0, span // step)
        def _(i):
            rows = pl.ds(pl.multiple_of(i * step, step), step)
            for k in range(slots):
                leaving[h][k, rows, :] = cache[h][chosen[1, k], rows, :]

    def first(h, i):
        peer = lax.rem(me + i, groups)
        rows = pl.ds(pl.multiple_of(peer * part, part), part)
        return pltpu.make_async_remote_copy(
            src_ref=leaving[h].at[:, rows, :],
            dst_ref=arrived[h].at[pl.ds(i * slots, slots)],
            send_sem=send1.at[h],
            recv_sem=recv1.at[h],
            device_id={"cand": peer},
        )

    for h in range(PARTS):
        spans[h].wait()
        pick(h)
        if h == 0:
            pl.semaphore_wait(barrier, groups + shares - 2)

        @pl.loop(1, groups)
        def _(t):
            first(h, lax.rem(t * 5, groups)).start()

        rows = pl.ds(pl.multiple_of(me * part, part), part)
        for k in range(slots):
            arrived[h][k] = leaving[h][k, rows, :]

    for load in loads:
        load.start()
    for load in loads[:3]:
        load.wait()
    lead = PER_KV * NEW_TOKEN_COUNT
    tokens = lax.broadcasted_iota(jnp.int32, (lead, NEW_TOKEN_COUNT), 0) % NEW_TOKEN_COUNT
    fresh = lax.broadcasted_iota(jnp.int32, (lead, NEW_TOKEN_COUNT), 1) <= tokens
    place = lax.broadcasted_iota(jnp.int32, (lead, CACHE_LENGTH), 1)

    @pl.loop(0, count)
    def _(c):
        heads = jnp.concatenate(
            [query[c, :, g * ATTN_DIM : (g + 1) * ATTN_DIM] for g in range(PER_KV)], axis=0
        )
        old = jnp.where(place < lengths[c], score(heads, kv[c, 0]) * SCALE, -1e30)
        now = jnp.where(fresh, score(heads, new[c, 0]) * SCALE, -1e30)
        peak = jnp.maximum(old.max(-1, keepdims=True), now.max(-1, keepdims=True))
        old = jnp.exp(old - peak)
        now = jnp.exp(now - peak)
        inverse = 1.0 / (old.sum(-1, keepdims=True) + now.sum(-1, keepdims=True))
        mixed = jnp.dot(
            (old * inverse).astype(jnp.bfloat16), kv[c, 1], preferred_element_type=jnp.float32
        ) + jnp.dot(
            (now * inverse).astype(jnp.bfloat16), new[c, 1], preferred_element_type=jnp.float32
        )
        mixed = mixed.astype(jnp.bfloat16)
        rows = pl.ds(pl.multiple_of(c * NEW_TOKEN_COUNT, NEW_TOKEN_COUNT), NEW_TOKEN_COUNT)
        for g in range(PER_KV):
            attn[rows, g * ATTN_DIM : (g + 1) * ATTN_DIM] = mixed[
                g * NEW_TOKEN_COUNT : (g + 1) * NEW_TOKEN_COUNT
            ]

    loads[3].wait()

    @pl.loop(0, shares)
    def _(p):
        columns = pl.ds(pl.multiple_of(p * width, width), width)
        pieces[p] = jnp.dot(
            attn[...], weight[:, columns], preferred_element_type=jnp.float32
        ).astype(jnp.bfloat16)

    def across(i):
        peer = lax.rem(share + i, shares)
        return pltpu.make_async_remote_copy(
            src_ref=pieces.at[peer],
            dst_ref=others.at[i - 1],
            send_sem=send3,
            recv_sem=recv3,
            device_id={"tp": peer},
        )

    @pl.loop(1, shares)
    def _(i):
        across(i).start()

    def second(h, i):
        peer = lax.rem(me + i, groups)
        rows = pl.ds(pl.multiple_of(h * span + me * part, part), part)
        return pltpu.make_async_remote_copy(
            src_ref=sorted_rows.at[pl.ds((h * groups + peer) * slots, slots)],
            dst_ref=moved_ref.at[:, rows, :],
            send_sem=send2,
            recv_sem=recv2,
            device_id={"cand": peer},
        )

    def keep(h):
        rows = pl.ds(pl.multiple_of(h * span + me * part, part), part)
        return pltpu.make_async_copy(
            sorted_rows.at[pl.ds((h * groups + me) * slots, slots)],
            moved_ref.at[:, rows, :],
            own_sem.at[h],
        )

    incoming = (groups - 1) * slots
    for h in range(PARTS):
        pltpu.make_async_copy(
            arrived[h].at[pl.ds(0, incoming)], arrived[h].at[pl.ds(slots, incoming)], recv1.at[h]
        ).wait()

        @pl.loop(0, groups)
        def _(g):
            for k in range(slots):
                s = g * slots + k
                sorted_rows[h * groups * slots + s] = arrived[h][chosen[0, s]]

        @pl.loop(1, groups)
        def _(t):
            second(h, lax.rem(t * 5, groups)).start()

        keep(h).start()

    pltpu.make_async_copy(others, others, recv3).wait()
    block = 32

    @pl.loop(0, out_ref.shape[0] // block)
    def _(r):
        rows = pl.ds(pl.multiple_of(r * block, block), block)
        total = pieces[share, rows, :].astype(jnp.float32)
        for i in range(shares - 1):
            total = total + others[i, rows, :].astype(jnp.float32)
        out_ref[rows, :] = total.astype(jnp.bfloat16)

    pltpu.make_async_copy(others, others, send3).wait()
    for h in range(PARTS):
        pltpu.make_async_copy(
            arrived[h].at[pl.ds(0, incoming)], arrived[h].at[pl.ds(slots, incoming)], send1.at[h]
        ).wait()
        keep(h).wait()
    everything = PARTS * incoming
    for sem in (send2, recv2):
        pltpu.make_async_copy(
            sorted_rows.at[pl.ds(0, everything)], sorted_rows.at[pl.ds(0, everything)], sem
        ).wait()


def exchange(groups, shares, slots, chosen, lengths, query, new, kv, weight, cache):
    count = query.shape[0]
    part = ROWS // groups // PARTS
    bf16 = jnp.bfloat16
    width = weight.shape[1] // shares
    lead = count * NEW_TOKEN_COUNT
    smem = pl.BlockSpec(memory_space=pltpu.SMEM)
    anywhere = pl.BlockSpec(memory_space=pl.ANY)
    dma = pltpu.SemaphoreType.DMA
    return pl.pallas_call(
        functools.partial(exchange_kernel, groups, shares, slots),
        out_shape=(
            jax.ShapeDtypeStruct((lead, width), bf16),
            jax.ShapeDtypeStruct((slots, ROWS, ATTN_DIM), bf16),
        ),
        in_specs=[smem] * 2 + [anywhere] * 5,
        out_specs=(pl.BlockSpec(memory_space=pltpu.VMEM), anywhere),
        scratch_shapes=[
            *[pltpu.VMEM((count, ROWS // PARTS, ATTN_DIM), bf16)] * PARTS,
            *[pltpu.VMEM((slots, ROWS // PARTS, ATTN_DIM), bf16)] * PARTS,
            *[pltpu.VMEM((groups * slots, part, ATTN_DIM), bf16)] * PARTS,
            pltpu.VMEM((PARTS * groups * slots, part, ATTN_DIM), bf16),
            pltpu.VMEM(query.shape, bf16),
            pltpu.VMEM(new.shape, bf16),
            pltpu.VMEM(kv.shape, bf16),
            pltpu.VMEM(weight.shape, bf16),
            pltpu.VMEM((lead, weight.shape[0]), bf16),
            pltpu.VMEM((shares, lead, width), bf16),
            pltpu.VMEM((shares - 1, lead, width), bf16),
            dma((PARTS,)),
            dma((4,)),
            dma((PARTS,)),
            dma((PARTS,)),
            dma,
            dma,
            dma,
            dma,
            dma((PARTS,)),
        ],
        compiler_params=pltpu.CompilerParams(
            collective_id=0, has_side_effects=True, vmem_limit_bytes=60 * 1024 * 1024
        ),
        name="exchange",
    )(chosen, lengths, query, new, kv, weight, cache)


def order_kernel(groups, count, slots, source, chosen):
    me = lax.axis_index("cand")
    total = source.shape[1]
    row = source[...]
    owner = lax.div(row, count)
    across = jnp.broadcast_to(owner.astype(jnp.float32), (total, total))
    before = lax.broadcasted_iota(jnp.int32, (total, total), 0) < lax.broadcasted_iota(
        jnp.int32, (total, total), 1
    )
    rank = jnp.where((across == across.T) & before, 1.0, 0.0).sum(0, keepdims=True)
    rank = rank.astype(jnp.int32)
    chosen[0:1, :] = lax.rem(me - owner + groups, groups) * slots + rank
    lane = lax.broadcasted_iota(jnp.int32, row.shape, 1)
    picked = jnp.zeros_like(row)
    local = lax.rem(row, count)
    for k in range(slots):
        one = jnp.where((owner == me) & (rank == k), local, 0).sum(1, keepdims=True)
        picked = jnp.where(lane == k, one, picked)
    chosen[1:2, :] = picked


def order(groups, count, slots, source):
    vmem = pl.BlockSpec(memory_space=pltpu.VMEM)
    return pl.pallas_call(
        functools.partial(order_kernel, groups, count, slots),
        out_shape=jax.ShapeDtypeStruct((2, source.shape[0]), jnp.int32),
        in_specs=[vmem],
        out_specs=vmem,
        name="order",
    )(source.reshape(1, -1))


def policy_kernel(
    source,
    lengths,
    moved,
    reward,
    new,
    query,
    kept,
    out,
    reward_out,
    held,
    passing,
    in_sem,
    out_sem,
    pass_sem,
):
    me = lax.axis_index("cand")
    slots = query.shape[0]
    loads = [pltpu.make_async_copy(moved.at[s], held.at[s], in_sem.at[s]) for s in range(slots)]
    stores = [pltpu.make_async_copy(held.at[s], kept.at[s], out_sem.at[s]) for s in range(slots)]
    for load in loads:
        load.start()
    come = pltpu.make_async_copy(reward, passing, pass_sem.at[0])
    go = pltpu.make_async_copy(passing, reward_out, pass_sem.at[1])
    come.start()
    asked = query[...].astype(jnp.float32)
    fresh = new[...]
    place = lax.broadcasted_iota(jnp.int32, (PER_KV, CACHE_LENGTH), 1)
    tile = 16
    within = lax.broadcasted_iota(jnp.int32, (tile, ATTN_DIM), 0)
    lines = []
    for s in range(slots):
        length = lengths[source[me * slots + s]]
        base = lax.div(length, tile) * tile
        loads[s].wait()
        for half in range(2):
            rows = pl.ds(pl.multiple_of(half * CACHE_LENGTH + base, tile), tile)
            held[s, rows, :] = jnp.where(
                within + base == length, fresh[s, half : half + 1, :], held[s, rows, :]
            )
        heads = jnp.concatenate(
            [asked[s : s + 1, g * ATTN_DIM : (g + 1) * ATTN_DIM] for g in range(PER_KV)], axis=0
        ).astype(jnp.bfloat16)
        found = score(heads, held[s, 0:CACHE_LENGTH, :]) * SCALE
        found = jnp.where(place <= length, found, -1e30)
        found = jnp.exp(found - found.max(-1, keepdims=True))
        found = found * (1.0 / found.sum(-1, keepdims=True))
        mixed = jnp.dot(
            found.astype(jnp.bfloat16),
            held[s, CACHE_LENGTH:ROWS, :],
            preferred_element_type=jnp.float32,
        )
        stores[s].start()
        lines.append(jnp.concatenate([mixed[g : g + 1] for g in range(PER_KV)], axis=1))
        if s == 0:
            come.wait()
            go.start()
    out[...] = jnp.concatenate(lines, axis=0).astype(jnp.bfloat16)
    for store in stores:
        store.wait()
    go.wait()


def policy(source, lengths, moved, reward, new, query):
    slots = query.shape[0]
    bf16 = jnp.bfloat16
    smem = pl.BlockSpec(memory_space=pltpu.SMEM)
    vmem = pl.BlockSpec(memory_space=pltpu.VMEM)
    anywhere = pl.BlockSpec(memory_space=pl.ANY)
    dma = pltpu.SemaphoreType.DMA
    return pl.pallas_call(
        policy_kernel,
        out_shape=(
            jax.ShapeDtypeStruct(moved.shape, bf16),
            jax.ShapeDtypeStruct(query.shape, bf16),
            jax.ShapeDtypeStruct(reward.shape, bf16),
        ),
        in_specs=[smem, smem, anywhere, anywhere, vmem, vmem],
        out_specs=(anywhere, vmem, anywhere),
        scratch_shapes=[
            pltpu.VMEM(moved.shape, bf16),
            pltpu.VMEM(reward.shape, bf16),
            dma((slots,)),
            dma((slots,)),
            dma((2,)),
        ],
        name="policy",
    )(source, lengths, moved, reward, new, query)


def body(
    groups,
    shares,
    reward_query,
    reward_new,
    reward_key_value_cache,
    reward_length,
    out_weight,
    policy_cache,
    policy_length,
    source,
    policy_query,
    policy_new,
):
    count = reward_query.shape[0]
    slots = policy_query.shape[0]
    reward, moved = exchange(
        groups,
        shares,
        slots,
        order(groups, count, slots, source),
        reward_length,
        reward_query,
        reward_new,
        reward_key_value_cache,
        out_weight,
        policy_cache.reshape(count, ROWS, ATTN_DIM),
    )
    compacted, policy_attn, reward_out = policy(
        source, policy_length, moved, reward, policy_new, policy_query
    )
    return (reward_out, compacted.reshape(slots, 2, CACHE_LENGTH, ATTN_DIM), policy_attn)


def solution(mesh):
    in_specs = (
        P("cand", None, "tp"),
        P("cand", None, None, "tp"),
        P("cand", None, None, "tp"),
        P("cand"),
        P("tp", None),
        P("cand", None, None, "tp"),
        P(),
        P(),
        P("cand", "tp"),
        P("cand", None, "tp"),
    )
    out_specs = (P("cand", "tp"), P("cand", None, None, "tp"), P("cand", "tp"))
    return jax.shard_map(
        functools.partial(body, mesh.shape["cand"], mesh.shape["tp"]),
        mesh=mesh,
        in_specs=in_specs,
        out_specs=out_specs,
        check_vma=False,
    )
```

```python
import functools

import jax
import jax.numpy as jnp
from jax import lax
from jax.experimental import pallas as pl
from jax.experimental.pallas import tpu as pltpu
from jax.sharding import PartitionSpec as P

ASKING_UNITS = 64
SHARED_KV_UNITS = 8
ATTN_DIM = 128
NEW_TOKEN_COUNT = 32
CACHE_LENGTH = 768
PER_KV = ASKING_UNITS // SHARED_KV_UNITS
ROWS = 2 * CACHE_LENGTH
SCALE = ATTN_DIM ** (-0.5)
PARTS = 3


def score(rows, keys):
    return lax.dot_general(
        rows, keys, (((1,), (1,)), ((), ())), preferred_element_type=jnp.float32
    )


def exchange_kernel(
    groups,
    shares,
    slots,
    chosen,
    lengths,
    query_hbm,
    new_hbm,
    kv_hbm,
    weight_hbm,
    cache_hbm,
    out_ref,
    moved_ref,
    cache0,
    cache1,
    cache2,
    leaving0,
    leaving1,
    leaving2,
    arrived0,
    arrived1,
    arrived2,
    sorted_rows,
    query,
    new,
    kv,
    weight,
    attn,
    pieces,
    others,
    span_sem,
    load_sem,
    send1,
    recv1,
    send2,
    recv2,
    send3,
    recv3,
    own_sem,
):
    cache = (cache0, cache1, cache2)
    leaving = (leaving0, leaving1, leaving2)
    arrived = (arrived0, arrived1, arrived2)
    me = lax.axis_index("cand")
    share = lax.axis_index("tp")
    span = ROWS // PARTS
    part = span // groups
    count = query.shape[0]
    width = pieces.shape[2]

    spans = [
        pltpu.make_async_copy(
            cache_hbm.at[:, pl.ds(h * span, span), :], cache[h], span_sem.at[h]
        )
        for h in range(PARTS)
    ]
    loads = [
        pltpu.make_async_copy(query_hbm, query, load_sem.at[0]),
        pltpu.make_async_copy(new_hbm, new, load_sem.at[1]),
        pltpu.make_async_copy(kv_hbm, kv, load_sem.at[2]),
        pltpu.make_async_copy(weight_hbm, weight, load_sem.at[3]),
    ]
    for load in spans:
        load.start()

    barrier = pltpu.get_barrier_semaphore()

    @pl.loop(1, groups)
    def _(i):
        pl.semaphore_signal(barrier, inc=1, device_id={"cand": lax.rem(me + i, groups)})

    @pl.loop(1, shares)
    def _(i):
        pl.semaphore_signal(barrier, inc=1, device_id={"tp": lax.rem(share + i, shares)})

    step = 128

    def pick(h):
        @pl.loop(0, span // step)
        def _(i):
            rows = pl.ds(pl.multiple_of(i * step, step), step)
            for k in range(slots):
                leaving[h][k, rows, :] = cache[h][chosen[1, k], rows, :]

    def first(h, i):
        peer = lax.rem(me + i, groups)
        rows = pl.ds(pl.multiple_of(peer * part, part), part)
        return pltpu.make_async_remote_copy(
            src_ref=leaving[h].at[:, rows, :],
            dst_ref=arrived[h].at[pl.ds(i * slots, slots)],
            send_sem=send1.at[h],
            recv_sem=recv1.at[h],
            device_id={"cand": peer},
        )

    for h in range(PARTS):
        spans[h].wait()
        pick(h)
        if h == 0:
            pl.semaphore_wait(barrier, groups + shares - 2)

        @pl.loop(1, groups)
        def _(t):
            first(h, lax.rem(t * 5, groups)).start()

        rows = pl.ds(pl.multiple_of(me * part, part), part)
        for k in range(slots):
            arrived[h][k] = leaving[h][k, rows, :]

    for load in loads:
        load.start()
    for load in loads[:3]:
        load.wait()
    lead = PER_KV * NEW_TOKEN_COUNT
    tokens = lax.broadcasted_iota(jnp.int32, (lead, NEW_TOKEN_COUNT), 0) % NEW_TOKEN_COUNT
    fresh = lax.broadcasted_iota(jnp.int32, (lead, NEW_TOKEN_COUNT), 1) <= tokens
    place = lax.broadcasted_iota(jnp.int32, (lead, CACHE_LENGTH), 1)

    @pl.loop(0, count)
    def _(c):
        heads = jnp.concatenate(
            [query[c, :, g * ATTN_DIM : (g + 1) * ATTN_DIM] for g in range(PER_KV)], axis=0
        )
        old = jnp.where(place < lengths[c], score(heads, kv[c, 0]) * SCALE, -1e30)
        now = jnp.where(fresh, score(heads, new[c, 0]) * SCALE, -1e30)
        peak = jnp.maximum(old.max(-1, keepdims=True), now.max(-1, keepdims=True))
        old = jnp.exp(old - peak)
        now = jnp.exp(now - peak)
        inverse = 1.0 / (old.sum(-1, keepdims=True) + now.sum(-1, keepdims=True))
        mixed = jnp.dot(
            (old * inverse).astype(jnp.bfloat16), kv[c, 1], preferred_element_type=jnp.float32
        ) + jnp.dot(
            (now * inverse).astype(jnp.bfloat16), new[c, 1], preferred_element_type=jnp.float32
        )
        mixed = mixed.astype(jnp.bfloat16)
        rows = pl.ds(pl.multiple_of(c * NEW_TOKEN_COUNT, NEW_TOKEN_COUNT), NEW_TOKEN_COUNT)
        for g in range(PER_KV):
            attn[rows, g * ATTN_DIM : (g + 1) * ATTN_DIM] = mixed[
                g * NEW_TOKEN_COUNT : (g + 1) * NEW_TOKEN_COUNT
            ]

    loads[3].wait()

    @pl.loop(0, shares)
    def _(p):
        columns = pl.ds(pl.multiple_of(p * width, width), width)
        pieces[p] = jnp.dot(
            attn[...], weight[:, columns], preferred_element_type=jnp.float32
        ).astype(jnp.bfloat16)

    def across(i):
        peer = lax.rem(share + i, shares)
        return pltpu.make_async_remote_copy(
            src_ref=pieces.at[peer],
            dst_ref=others.at[i - 1],
            send_sem=send3,
            recv_sem=recv3,
            device_id={"tp": peer},
        )

    @pl.loop(1, shares)
    def _(i):
        across(i).start()

    def second(h, i):
        peer = lax.rem(me + i, groups)
        rows = pl.ds(pl.multiple_of(h * span + me * part, part), part)
        return pltpu.make_async_remote_copy(
            src_ref=sorted_rows.at[pl.ds((h * groups + peer) * slots, slots)],
            dst_ref=moved_ref.at[:, rows, :],
            send_sem=send2,
            recv_sem=recv2,
            device_id={"cand": peer},
        )

    def keep(h):
        rows = pl.ds(pl.multiple_of(h * span + me * part, part), part)
        return pltpu.make_async_copy(
            sorted_rows.at[pl.ds((h * groups + me) * slots, slots)],
            moved_ref.at[:, rows, :],
            own_sem.at[h],
        )

    incoming = (groups - 1) * slots
    for h in range(PARTS):
        pltpu.make_async_copy(
            arrived[h].at[pl.ds(0, incoming)], arrived[h].at[pl.ds(slots, incoming)], recv1.at[h]
        ).wait()

        @pl.loop(0, groups)
        def _(g):
            for k in range(slots):
                s = g * slots + k
                sorted_rows[h * groups * slots + s] = arrived[h][chosen[0, s]]

        @pl.loop(1, groups)
        def _(t):
            second(h, lax.rem(t * 5, groups)).start()

        keep(h).start()

    pltpu.make_async_copy(others, others, recv3).wait()
    block = 32

    @pl.loop(0, out_ref.shape[0] // block)
    def _(r):
        rows = pl.ds(pl.multiple_of(r * block, block), block)
        total = pieces[share, rows, :].astype(jnp.float32)
        for i in range(shares - 1):
            total = total + others[i, rows, :].astype(jnp.float32)
        out_ref[rows, :] = total.astype(jnp.bfloat16)

    pltpu.make_async_copy(others, others, send3).wait()
    for h in range(PARTS):
        pltpu.make_async_copy(
            arrived[h].at[pl.ds(0, incoming)], arrived[h].at[pl.ds(slots, incoming)], send1.at[h]
        ).wait()
        keep(h).wait()
    everything = PARTS * incoming
    for sem in (send2, recv2):
        pltpu.make_async_copy(
            sorted_rows.at[pl.ds(0, everything)], sorted_rows.at[pl.ds(0, everything)], sem
        ).wait()


def exchange(groups, shares, slots, chosen, lengths, query, new, kv, weight, cache):
    count = query.shape[0]
    part = ROWS // groups // PARTS
    bf16 = jnp.bfloat16
    width = weight.shape[1] // shares
    lead = count * NEW_TOKEN_COUNT
    smem = pl.BlockSpec(memory_space=pltpu.SMEM)
    anywhere = pl.BlockSpec(memory_space=pl.ANY)
    dma = pltpu.SemaphoreType.DMA
    return pl.pallas_call(
        functools.partial(exchange_kernel, groups, shares, slots),
        out_shape=(
            jax.ShapeDtypeStruct((lead, width), bf16),
            jax.ShapeDtypeStruct((slots, ROWS, ATTN_DIM), bf16),
        ),
        in_specs=[smem] * 2 + [anywhere] * 5,
        out_specs=(pl.BlockSpec(memory_space=pltpu.VMEM), anywhere),
        scratch_shapes=[
            *[pltpu.VMEM((count, ROWS // PARTS, ATTN_DIM), bf16)] * PARTS,
            *[pltpu.VMEM((slots, ROWS // PARTS, ATTN_DIM), bf16)] * PARTS,
            *[pltpu.VMEM((groups * slots, part, ATTN_DIM), bf16)] * PARTS,
            pltpu.VMEM((PARTS * groups * slots, part, ATTN_DIM), bf16),
            pltpu.VMEM(query.shape, bf16),
            pltpu.VMEM(new.shape, bf16),
            pltpu.VMEM(kv.shape, bf16),
            pltpu.VMEM(weight.shape, bf16),
            pltpu.VMEM((lead, weight.shape[0]), bf16),
            pltpu.VMEM((shares, lead, width), bf16),
            pltpu.VMEM((shares - 1, lead, width), bf16),
            dma((PARTS,)),
            dma((4,)),
            dma((PARTS,)),
            dma((PARTS,)),
            dma,
            dma,
            dma,
            dma,
            dma((PARTS,)),
        ],
        compiler_params=pltpu.CompilerParams(
            collective_id=0, has_side_effects=True, vmem_limit_bytes=60 * 1024 * 1024
        ),
        name="exchange",
    )(chosen, lengths, query, new, kv, weight, cache)


def order_kernel(groups, count, slots, source, chosen):
    me = lax.axis_index("cand")
    total = source.shape[1]
    row = source[...]
    owner = lax.div(row, count)
    across = jnp.broadcast_to(owner.astype(jnp.float32), (total, total))
    before = lax.broadcasted_iota(jnp.int32, (total, total), 0) < lax.broadcasted_iota(
        jnp.int32, (total, total), 1
    )
    rank = jnp.where((across == across.T) & before, 1.0, 0.0).sum(0, keepdims=True)
    rank = rank.astype(jnp.int32)
    chosen[0:1, :] = lax.rem(me - owner + groups, groups) * slots + rank
    lane = lax.broadcasted_iota(jnp.int32, row.shape, 1)
    picked = jnp.zeros_like(row)
    local = lax.rem(row, count)
    for k in range(slots):
        one = jnp.where((owner == me) & (rank == k), local, 0).sum(1, keepdims=True)
        picked = jnp.where(lane == k, one, picked)
    chosen[1:2, :] = picked


def order(groups, count, slots, source):
    vmem = pl.BlockSpec(memory_space=pltpu.VMEM)
    return pl.pallas_call(
        functools.partial(order_kernel, groups, count, slots),
        out_shape=jax.ShapeDtypeStruct((2, source.shape[0]), jnp.int32),
        in_specs=[vmem],
        out_specs=vmem,
        name="order",
    )(source.reshape(1, -1))


def policy_kernel(
    source,
    lengths,
    moved,
    reward,
    new,
    query,
    kept,
    out,
    reward_out,
    held,
    passing,
    in_sem,
    out_sem,
    pass_sem,
):
    me = lax.axis_index("cand")
    slots = query.shape[0]
    loads = [pltpu.make_async_copy(moved.at[s], held.at[s], in_sem.at[s]) for s in range(slots)]
    stores = [pltpu.make_async_copy(held.at[s], kept.at[s], out_sem.at[s]) for s in range(slots)]
    for load in loads:
        load.start()
    come = pltpu.make_async_copy(reward, passing, pass_sem.at[0])
    go = pltpu.make_async_copy(passing, reward_out, pass_sem.at[1])
    come.start()
    asked = query[...].astype(jnp.float32)
    fresh = new[...]
    place = lax.broadcasted_iota(jnp.int32, (slots * PER_KV, CACHE_LENGTH), 1)
    tile = 16
    within = lax.broadcasted_iota(jnp.int32, (tile, ATTN_DIM), 0)
    ends, scores = [], []
    for s in range(slots):
        length = lengths[source[me * slots + s]]
        ends.append(jnp.full((PER_KV, CACHE_LENGTH), length, jnp.int32))
        base = lax.div(length, tile) * tile
        loads[s].wait()
        for half in range(2):
            rows = pl.ds(pl.multiple_of(half * CACHE_LENGTH + base, tile), tile)
            held[s, rows, :] = jnp.where(
                within + base == length, fresh[s, half : half + 1, :], held[s, rows, :]
            )
        heads = jnp.concatenate(
            [asked[s : s + 1, g * ATTN_DIM : (g + 1) * ATTN_DIM] for g in range(PER_KV)], axis=0
        ).astype(jnp.bfloat16)
        scores.append(score(heads, held[s, 0:CACHE_LENGTH, :]) * SCALE)
        if s == 0:
            come.wait()
            go.start()
        if s > 0:
            stores[s - 1].start()
    stores[slots - 1].start()
    found = jnp.concatenate(scores, axis=0)
    found = jnp.where(place <= jnp.concatenate(ends, axis=0), found, -1e30)
    found = jnp.exp(found - found.max(-1, keepdims=True))
    found = (found * (1.0 / found.sum(-1, keepdims=True))).astype(jnp.bfloat16)
    lines = []
    for s in range(slots):
        mixed = jnp.dot(
            found[s * PER_KV : (s + 1) * PER_KV],
            held[s, CACHE_LENGTH:ROWS, :],
            preferred_element_type=jnp.float32,
        )
        lines.append(jnp.concatenate([mixed[g : g + 1] for g in range(PER_KV)], axis=1))
    out[...] = jnp.concatenate(lines, axis=0).astype(jnp.bfloat16)
    for store in stores:
        store.wait()
    go.wait()


def policy(source, lengths, moved, reward, new, query):
    slots = query.shape[0]
    bf16 = jnp.bfloat16
    smem = pl.BlockSpec(memory_space=pltpu.SMEM)
    vmem = pl.BlockSpec(memory_space=pltpu.VMEM)
    anywhere = pl.BlockSpec(memory_space=pl.ANY)
    dma = pltpu.SemaphoreType.DMA
    return pl.pallas_call(
        policy_kernel,
        out_shape=(
            jax.ShapeDtypeStruct(moved.shape, bf16),
            jax.ShapeDtypeStruct(query.shape, bf16),
            jax.ShapeDtypeStruct(reward.shape, bf16),
        ),
        in_specs=[smem, smem, anywhere, anywhere, vmem, vmem],
        out_specs=(anywhere, vmem, anywhere),
        scratch_shapes=[
            pltpu.VMEM(moved.shape, bf16),
            pltpu.VMEM(reward.shape, bf16),
            dma((slots,)),
            dma((slots,)),
            dma((2,)),
        ],
        name="policy",
    )(source, lengths, moved, reward, new, query)


def body(
    groups,
    shares,
    reward_query,
    reward_new,
    reward_key_value_cache,
    reward_length,
    out_weight,
    policy_cache,
    policy_length,
    source,
    policy_query,
    policy_new,
):
    count = reward_query.shape[0]
    slots = policy_query.shape[0]
    reward, moved = exchange(
        groups,
        shares,
        slots,
        order(groups, count, slots, source),
        reward_length,
        reward_query,
        reward_new,
        reward_key_value_cache,
        out_weight,
        policy_cache.reshape(count, ROWS, ATTN_DIM),
    )
    compacted, policy_attn, reward_out = policy(
        source, policy_length, moved, reward, policy_new, policy_query
    )
    return (reward_out, compacted.reshape(slots, 2, CACHE_LENGTH, ATTN_DIM), policy_attn)


def solution(mesh):
    in_specs = (
        P("cand", None, "tp"),
        P("cand", None, None, "tp"),
        P("cand", None, None, "tp"),
        P("cand"),
        P("tp", None),
        P("cand", None, None, "tp"),
        P(),
        P(),
        P("cand", "tp"),
        P("cand", None, "tp"),
    )
    out_specs = (P("cand", "tp"), P("cand", None, None, "tp"), P("cand", "tp"))
    return jax.shard_map(
        functools.partial(body, mesh.shape["cand"], mesh.shape["tp"]),
        mesh=mesh,
        in_specs=in_specs,
        out_specs=out_specs,
        check_vma=False,
    )
```
